32 devices in a mesh: slab: 8 (over z, core), loop: 4 (over y, x).
Axes of the slice: x: 2, y: 2, z: 4, core: 2. Of those that a mesh axis runs over, the one named last changes fastest.
Arguments:
- doc_pool: bfloat16 [8, 4, 256, 4096], P('slab', 'loop'), may hold values from -6 to 6
- cand_owner: int32 [8, 4, 16, 1], P('slab', 'loop'), may hold values from 0 to 7; in each aligned block of 16 rows (0 to 15, 16 to 31, ..., all dimensions but the last counted through in order) at most 4 rows name the same one
- cand_row: int32 [8, 4, 16], P('slab', 'loop'), may hold values from 0 to 255
- elements: bfloat16 [8, 4, 2048, 4096], P('slab', 'loop'), may hold values from -6 to 6
- coverage: float32 [8, 4, 2048], P('slab', 'loop'), may hold values from -0.5 to 1.5
- elem_weight: float32 [8, 4, 2048], P('slab', 'loop'), may hold values from 1 to 10
Outputs:
- gains: float32 [8, 4, 16], P('slab', 'loop')
The draws below stay inside these ranges and needn't reach their ends.
Inputs may be any that keep to these rules, and one draw needn't show every extreme that they name: `cand_owner`: among the candidates of one device, at most 4 name the same owner; some owner is named exactly 4 times.
All inputs are finite; a program needn't handle non-finite values.
Results may differ from the reference program's by a relative error of at most 0.0003.
Values may be sent and summed in bfloat16 or wider, within the bound.
A program may use at most 128 MiB of HBM per device.

```python
import math
import jax
import jax.numpy as jnp
import numpy as np
from jax import lax

D = 4096
CB = 128
ELEM_DEV = 2048
POOL_DEV = 256
CAP = 4
ELEMS = 65536
N_SLAB = 8
N_LOOP = 4


def plant(drawn, key, least, largest):
    extent = drawn.shape
    index_at = [jax.random.randint(jax.random.fold_in(key, axis), (), 0, extent[axis]) for axis in range(len(extent))]
    drawn = drawn.at[tuple(index_at)].set(least)
    longest = extent.index(max(extent))
    index_at[longest] = (index_at[longest] + 1) % extent[longest]
    return drawn.at[tuple(index_at)].set(largest)


def level_of(rng, extent, cuts, smallest, top_value):
    def one(axis_at, parts):
        heights = jax.random.uniform(jax.random.fold_in(jax.random.fold_in(rng, 6), axis_at), (parts,), jnp.float32, smallest / len(cuts), top_value / len(cuts))
        return jnp.repeat(jnp.exp(heights), extent[axis_at] // parts).reshape((-1,) + (1,) * (len(extent) - axis_at - 1))

    factor_of = one(*cuts[0])
    for cut in cuts[1:]:
        factor_of = factor_of * one(*cut)
    return factor_of


def deal_out(key, own, number, rows, count, top, most, skew):
    ranking = jax.random.permutation(key, count)
    packed, common = portions_of(count, rows * top, most, skew, True), portions_of(count, rows * top, most, skew, False)
    places = jnp.arange(count)

    def named(lengths, rotation):
        used = int((lengths > 0).sum())
        fixed = max(1, used // 4)
        shifted = fixed + (places - fixed + rotation * (used - fixed)) % max(1, count - fixed)
        return jnp.zeros((count,), jnp.int32).at[ranking[jnp.where(places < fixed, places, shifted)]].set(jnp.asarray(lengths, jnp.int32))

    lengths = jnp.where(number % 4 == 0, named(packed, number // 4), named(common, number - number // 4 - 1))
    mixed = jax.random.permutation(jax.random.fold_in(own, 3), count)
    source_of, taker = mixed[0:count // 2 * 2:2], mixed[1:count // 2 * 2:2]
    margin = jnp.minimum(lengths[source_of] - 1, most - lengths[taker]) // 2
    margin = jnp.where((source_of == ranking[0]) | (taker == ranking[0]) | (lengths[taker] == 0), 0, jnp.maximum(margin, 0))
    shifted = jax.random.randint(jax.random.fold_in(own, 4), (count // 2,), 0, 1 << 20) % (margin + 1)
    lengths = lengths.at[source_of].add(-shifted).at[taker].add(shifted)
    labels = jnp.searchsorted(jnp.cumsum(lengths), jnp.arange(rows * top), side="right").astype(jnp.int32)
    table = labels.reshape(top, rows).T
    table = table[jax.random.permutation(jax.random.fold_in(own, 1), rows)]
    rotation = jax.random.randint(jax.random.fold_in(own, 2), (rows, 1), 0, top)
    return jnp.take_along_axis(table, (jnp.arange(top)[None, :] + rotation) % top, axis=1)


def portions_of(amount, total, bound, lean, full):
    weights = [(1 << 20) // math.isqrt(standing ** lean) + 1 for standing in range(1, amount + 1)]
    largest = bound if full else min(bound, max(-(-total // amount), total * weights[0] // sum(weights)))
    least = 1 if total - largest >= amount - 1 else 0
    holding, rest = [largest] + [least] * (amount - 1), total - largest - least * (amount - 1)
    while rest > 0:
        candidates = [i for i in range(1, amount) if holding[i] < largest] or [i for i in range(1, amount) if holding[i] < bound]
        pool, budget = sum([weights[i] for i in candidates]), rest
        for i in candidates:
            extra = min(bound - holding[i], max(1, budget * weights[i] // pool), rest)
            holding[i] = holding[i] + extra
            rest = rest - extra
    return np.array(holding)


def centred(stream_key, extent, width, bound, pieces=(), kind=jnp.bfloat16):
    gain = level_of(stream_key, extent, pieces, -0.22, 0.18) if pieces else 1.0
    values = jax.random.normal(stream_key, extent, jnp.float32) * width * gain
    return jnp.minimum(jnp.maximum(values, -bound), bound).astype(kind)


def setup_inputs(seed: int = 0) -> dict:
    key_of = jax.random.split(jax.random.key(seed), 7)
    doc_pool = centred(key_of[0], (N_SLAB, N_LOOP, POOL_DEV, D), 1.0, 6.0, ((0, 8), (1, 4)))
    cand_owner_keys = jax.random.split(jax.random.fold_in(key_of[1], 1), N_SLAB * N_LOOP * (CB // N_SLAB) // (CB // N_SLAB))
    cand_owner_turns = jax.random.permutation(jax.random.fold_in(key_of[1], 3), N_SLAB * N_LOOP * (CB // N_SLAB) // (CB // N_SLAB))
    cand_owner = jax.vmap(lambda own, number: deal_out(jax.random.fold_in(key_of[1], 2), own, number, CB // N_SLAB, N_SLAB, 1, CAP, 2))(cand_owner_keys, cand_owner_turns).reshape((N_SLAB, N_LOOP, CB // N_SLAB, 1))
    cand_row = plant(jax.random.randint(key_of[2], (N_SLAB, N_LOOP, CB // N_SLAB), 0, POOL_DEV), jax.random.fold_in(key_of[2], 1), 0, POOL_DEV - 1).astype(jnp.int32)
    elements = centred(key_of[3], (N_SLAB, N_LOOP, ELEM_DEV, D), 1.0, 6.0, ((0, 8), (1, 4)))
    coverage = jnp.clip(-0.5 + 2.0 * jax.random.uniform(key_of[4], (N_SLAB, N_LOOP, ELEM_DEV), jnp.float32) ** level_of(key_of[4], (N_SLAB, N_LOOP, ELEM_DEV), ((0, 8), (1, 4)), -0.2, 0.2), -0.5, 1.5)
    elem_weight = jnp.clip(jnp.exp(math.log(10.0) - 2.3025851 * jax.random.uniform(key_of[5], (N_SLAB, N_LOOP, ELEM_DEV), jnp.float32) ** level_of(key_of[5], (N_SLAB, N_LOOP, ELEM_DEV), ((0, 8), (1, 4)), -0.2, 0.2)), 1.0, 10.0)
    return dict(doc_pool=doc_pool, cand_owner=cand_owner, cand_row=cand_row, elements=elements, coverage=coverage, elem_weight=elem_weight)


def reference(doc_pool, cand_owner, cand_row, elements, coverage, elem_weight):
    owner_ids = cand_owner[..., 0]
    column_ids = jnp.broadcast_to(jnp.arange(N_LOOP, dtype=jnp.int32)[None, :, None], owner_ids.shape)
    cand_emb = doc_pool[owner_ids, column_ids, cand_row]
    cand_flat = cand_emb.reshape(-1, D)
    sim_scale = float(D) ** -0.5
    shard_elems = elements.reshape(N_SLAB * N_LOOP, ELEM_DEV, D)
    shard_cover = coverage.reshape(N_SLAB * N_LOOP, ELEM_DEV)
    shard_weight = elem_weight.reshape(N_SLAB * N_LOOP, ELEM_DEV)

    def accumulate(running, shard):
        docs, cover_part, weight_part = shard
        scores = jnp.dot(docs, cand_flat.T, preferred_element_type=jnp.float32) * sim_scale
        term = jnp.sum(weight_part[:, None] * jnp.maximum(scores - cover_part[:, None], 0.0), axis=0)
        return running + term, None

    init = jnp.zeros((cand_flat.shape[0],), jnp.float32)
    running, _ = lax.scan(accumulate, init, (shard_elems, shard_cover, shard_weight))
    gains = running / float(ELEMS)
    return gains.reshape(owner_ids.shape)
```

```python
import functools

import jax
import jax.numpy as jnp
from jax import lax
from jax.experimental import pallas as pl
from jax.experimental.pallas import tpu as pltpu
from jax.sharding import PartitionSpec as P

MESH = pl.DeviceIdType.MESH
LANES = 128
SUB = 8
CHUNKS = 8
RING_LAG = 2
HOP_LAG = 2
LAST_LAG = 1


def kernel(
    dims,
    owner_ref, row_ref, cover_ref, weight_ref, pool_hbm, docs_hbm,
    out_ref,
    pool, docs, req_out, req_in, picked, fetched, cand, acc, part, terms,
    pool_sem, docs_sem, req_send, req_recv, pick_send, pick_recv,
    cand_send, relay_send, line_recv, ring_recv, pair_recv, term_send, term_recv,
):
    slabs, loops, share, cap, chunks, chunk, tile, total_docs, scale = dims
    lines = slabs // 2
    units = slabs * loops
    rows_pool = pool.shape[0]
    n_docs = docs.shape[0]
    slab = lax.axis_index("slab")
    loop = lax.axis_index("loop")
    line = slab // 2
    core = lax.rem(slab, 2)
    me = slab * loops + loop
    half = loops // 2
    reach_even, reach_odd = half, loops - 1 - half
    relayed = lines == 4

    def loop_of(pos):
        return jnp.where(pos < half, 2 * pos, 2 * (loops - 1 - pos) + 1)

    def pos_of(at):
        return jnp.where(lax.rem(at, 2) == 0, at // 2, loops - 1 - at // 2)

    here = pos_of(loop)
    ahead = loop_of(lax.rem(here + 1, loops))
    behind = loop_of(lax.rem(here + loops - 1, loops))

    pool_copy = pltpu.make_async_copy(pool_hbm, pool, pool_sem.at[0])
    docs_copy = pltpu.make_async_copy(docs_hbm, docs, docs_sem.at[0])

    barrier = pltpu.get_barrier_semaphore()

    def greet(device):
        pl.semaphore_signal(barrier, inc=1, device_id=device, device_id_type=MESH)

    for d in range(1, slabs):
        greet((lax.rem(slab + d, slabs), loop))
    for d in range(1, loops):
        greet((slab, lax.rem(loop + d, loops)))
    pool_copy.start()
    docs_copy.start()

    owner_row = owner_ref[...]
    row_row = row_ref[...]
    down = lax.broadcasted_iota(jnp.int32, (share, share), 0)
    across = lax.broadcasted_iota(jnp.int32, (share, share), 1)
    wide = jnp.broadcast_to(owner_row, (share, share)).astype(jnp.float32)
    owner_col = jnp.sum(jnp.where(down == across, wide, 0.0), axis=1, keepdims=True)
    rank_row = jnp.sum(
        jnp.where((owner_col == wide) & (down < across), 1.0, 0.0), axis=0, keepdims=True
    )
    owner_f = owner_row.astype(jnp.float32)
    asked_row = owner_f * SUB + rank_row
    slot_row = owner_f * cap + rank_row
    slot_col = jnp.sum(
        jnp.where(down == across, jnp.broadcast_to(slot_row, (share, share)), 0.0),
        axis=1, keepdims=True,
    )
    place = lax.broadcasted_iota(jnp.int32, (slabs * SUB, share), 0).astype(jnp.float32)
    asked = jnp.sum(
        jnp.where(place == asked_row, row_row.astype(jnp.float32), 0.0), axis=1, keepdims=True
    )
    req_out[...] = jnp.broadcast_to(asked, (slabs * SUB, LANES)).astype(jnp.int32).reshape(
        slabs, SUB, LANES
    )
    choose = jnp.where(
        slot_col == lax.broadcasted_iota(jnp.int32, (share, slabs * cap), 1).astype(jnp.float32),
        1.0, 0.0,
    ).astype(jnp.bfloat16)

    pl.semaphore_wait(barrier, slabs + loops - 2)

    def remote(src, dst, send, recv, device):
        return pltpu.make_async_remote_copy(
            src_ref=src, dst_ref=dst, send_sem=send, recv_sem=recv,
            device_id=device, device_id_type=MESH,
        )

    def settle(ref, sem):
        pltpu.make_async_copy(ref, ref, sem).wait()

    for d in range(1, slabs):
        other = lax.rem(slab + d, slabs)
        remote(
            req_out.at[other], req_in.at[slab], req_send.at[0], req_recv.at[0], (other, loop)
        ).start()
    req_in[slab] = req_out[slab]
    pool_copy.wait()
    settle(req_in.at[pl.ds(0, slabs - 1)], req_recv.at[0])

    wanted = req_in[...].reshape(slabs * SUB, LANES)
    lane = lax.broadcasted_iota(jnp.int32, (slabs * SUB, LANES), 1)
    pick = jnp.concatenate(
        [
            jnp.where(wanted == lane + b * LANES, 1.0, 0.0).astype(jnp.bfloat16)
            for b in range(rows_pool // LANES)
        ],
        axis=1,
    )

    def gather(k):
        rows = jnp.dot(
            pick, pool[:, k * chunk:(k + 1) * chunk], preferred_element_type=jnp.float32
        )
        for r in range(slabs):
            picked[k, r] = rows[r * SUB:r * SUB + cap].astype(jnp.bfloat16)
        for d in range(1, slabs):
            other = lax.rem(slab + d, slabs)
            remote(
                picked.at[k, other], fetched.at[k, slab], pick_send.at[0], pick_recv.at[k],
                (other, loop),
            ).start()
        fetched[k, slab] = picked[k, slab]

    def to_ring(k, block, e, way):
        slot = e - 1 if way == 0 else jnp.where(core == 0, reach_even, reach_odd) + e - 1
        remote(
            block, block, cand_send.at[0], ring_recv.at[k, slot],
            (slab, ahead if way == 0 else behind),
        ).start()

    def to_pair(k, pos):
        block = cand.at[k, core, pos]
        remote(
            block, block, cand_send.at[0], pair_recv.at[k], (2 * line + 1 - core, loop)
        ).start()

    edge = (line == 0) | (line == lines - 1)

    def own(k):
        settle(fetched.at[k, pl.ds(0, slabs - 1)], pick_recv.at[k])
        rows = jnp.concatenate(
            [fetched[k, o].astype(jnp.float32) for o in range(slabs)], axis=0
        ).astype(jnp.bfloat16)
        mine = jnp.dot(choose, rows, preferred_element_type=jnp.float32)
        cand[k, core, here, line] = mine.astype(jnp.bfloat16)
        block = cand.at[k, core, here, line]
        if relayed:
            targets = [
                jnp.where(edge, jnp.where(line == 0, 2, 1), lines - 1 - line),
                jnp.where(edge, jnp.where(line == 0, 1, 2), jnp.where(line == 1, 0, 3)),
            ]
        else:
            targets = [lax.rem(line + d, lines) for d in range(1, lines)]
        for to in targets:
            remote(
                block, block, cand_send.at[0], line_recv.at[k], (2 * to + core, loop)
            ).start()
        to_ring(k, block, 1, 0)
        to_ring(k, block, 1, 1)

    def column(k):
        settle(cand.at[k, 0, 0, pl.ds(0, lines - 1)], line_recv.at[k])
        if relayed:
            @pl.when(jnp.logical_not(edge))
            def _():
                block = cand.at[k, core, here, pl.ds(jnp.where(line == 1, 2, 0), 2)]
                remote(
                    block, block, relay_send.at[0], line_recv.at[k],
                    (2 * jnp.where(line == 1, 0, 3) + core, loop),
                ).start()
        for d in range(1, lines):
            block = cand.at[k, core, here, lax.rem(line + d, lines)]
            to_ring(k, block, 1, 0)
            to_ring(k, block, 1, 1)
        to_pair(k, here)

    def ring(k, e):
        for way in (0, 1):
            reach = (reach_even, reach_odd) if way == 0 else (reach_odd, reach_even)
            limit = jnp.where(core == 0, reach[0], reach[1])
            pos = lax.rem(here - e + loops if way == 0 else here + e, loops)
            block = cand.at[k, core, pos]

            def arrive(way=way, reach=reach, limit=limit, pos=pos, block=block):
                slot = e - 1 if way == 0 else jnp.where(core == 0, reach_even, reach_odd) + e - 1
                settle(block, ring_recv.at[k, slot])
                if e < min(reach):
                    to_ring(k, block, e + 1, way)
                elif e < max(reach):
                    @pl.when(e < limit)
                    def _():
                        to_ring(k, block, e + 1, way)
                to_pair(k, pos)

            if e <= min(reach):
                arrive()
            elif e <= max(reach):
                pl.when(e <= limit)(arrive)

    cover_cols = jnp.transpose(cover_ref[...])
    weight_cols = jnp.transpose(weight_ref[...])
    tiles = n_docs // tile

    def multiply(k, i):
        if k == 0 and i == 0:
            docs_copy.wait()
        share_all = cand[k].reshape(units * share, chunk)
        at = slice(i * tile, (i + 1) * tile)
        product = lax.dot_general(
            docs[at, k * chunk:(k + 1) * chunk], share_all, (((1,), (1,)), ((), ())),
            preferred_element_type=jnp.float32,
        )
        if k == 0:
            acc[at, :] = product
        elif k < chunks - 1:
            acc[at, :] += product
        else:
            scores = (acc[at, :] + product) * scale
            total = jnp.zeros((1, units * share), jnp.float32)
            for j in range(tile // LANES):
                col = i * (tile // LANES) + j
                s = scores[j * LANES:(j + 1) * LANES, :]
                gain = weight_cols[:, col:col + 1] * jnp.maximum(
                    s - cover_cols[:, col:col + 1], 0.0
                )
                total = total + jnp.sum(gain, axis=0, keepdims=True)
            return total

    for k in range(chunks):
        gather(k)
    for k in range(chunks):
        own(k)
    lags = [RING_LAG + HOP_LAG * (e - 1) for e in range(1, half + 1)]
    final = lags[-1] + LAST_LAG
    total = jnp.zeros((1, units * share), jnp.float32)
    for t in range(chunks + final):
        stages = []
        if t < chunks:
            stages.append(functools.partial(column, t))
        for e in range(1, half + 1):
            if 0 <= t - lags[e - 1] < chunks:
                stages.append(functools.partial(ring, t - lags[e - 1], e))
        done = t - final
        if done >= 0:
            settle(cand.at[done, 0], pair_recv.at[done])
        for n in range(max(tiles, len(stages))):
            if n < len(stages):
                stages[n]()
            if done >= 0 and n < tiles:
                gains = multiply(done, n)
                if gains is not None:
                    total = total + gains
    total = total / total_docs
    for r in range(units * share // LANES):
        part[r] = total[:, r * LANES:(r + 1) * LANES]

    def first_of(s, p):
        return ((lax.rem(s, 2) * loops + pos_of(p)) * lines + s // 2) * share

    for d in range(slabs):
        for e in range(loops):
            if d + e > 0:
                s, p = lax.rem(slab + d, slabs), lax.rem(loop + e, loops)
                remote(
                    part.at[first_of(s, p) // LANES], terms.at[me], term_send.at[0],
                    term_recv.at[0], (s, p),
                ).start()
    first = first_of(slab, loop)
    terms[me] = part[first // LANES]
    sent = 2 + (2 if relayed else lines - 1) + 2 * (lines - 1) + (loops - 3) * lines + loops * lines
    settle(docs.at[pl.ds(0, sent * share)], cand_send.at[0])
    if relayed:
        @pl.when(jnp.logical_not(edge))
        def _():
            settle(docs.at[pl.ds(0, 2 * share)], relay_send.at[0])
    settle(req_in.at[pl.ds(0, slabs - 1)], req_send.at[0])
    settle(picked.at[:, pl.ds(0, slabs - 1)], pick_send.at[0])
    settle(terms.at[pl.ds(0, units - 1)], term_recv.at[0])
    settle(terms.at[pl.ds(0, units - 1)], term_send.at[0])
    row = jnp.sum(terms[...], axis=0)
    mine = lax.broadcasted_iota(jnp.int32, (LANES, LANES), 0)
    to = lax.broadcasted_iota(jnp.int32, (LANES, LANES), 1)
    column_of = jnp.sum(
        jnp.where(mine == to, jnp.broadcast_to(row, (LANES, LANES)), 0.0), axis=1, keepdims=True
    )
    moved = jnp.sum(
        jnp.where(mine == to + lax.rem(first, LANES), column_of, 0.0), axis=0, keepdims=True
    )
    out_ref[...] = moved[:, :share]


def body(dims, doc_pool, cand_owner, cand_row, elements, coverage, elem_weight):
    slabs, loops, share, cap, chunks, chunk, tile, _, _ = dims
    pool_rows, width = doc_pool.shape[2:]
    n_docs = elements.shape[2]
    units = slabs * loops
    vmem = pl.BlockSpec(memory_space=pltpu.VMEM)
    hbm = pl.BlockSpec(memory_space=pl.ANY)
    dma = pltpu.SemaphoreType.DMA
    out = pl.pallas_call(
        functools.partial(kernel, dims),
        out_shape=jax.ShapeDtypeStruct((1, share), jnp.float32),
        in_specs=[vmem, vmem, vmem, vmem, hbm, hbm],
        out_specs=vmem,
        scratch_shapes=[
            pltpu.VMEM((pool_rows, width), jnp.bfloat16),
            pltpu.VMEM((n_docs, width), jnp.bfloat16),
            pltpu.VMEM((slabs, SUB, LANES), jnp.int32),
            pltpu.VMEM((slabs, SUB, LANES), jnp.int32),
            pltpu.VMEM((chunks, slabs, cap, chunk), jnp.bfloat16),
            pltpu.VMEM((chunks, slabs, cap, chunk), jnp.bfloat16),
            pltpu.VMEM((chunks, 2, loops, slabs // 2, share, chunk), jnp.bfloat16),
            pltpu.VMEM((n_docs, units * share), jnp.float32),
            pltpu.VMEM((units * share // LANES, 1, LANES), jnp.float32),
            pltpu.VMEM((units, 1, LANES), jnp.float32),
            dma((1,)),
            dma((1,)),
            dma((1,)),
            dma((1,)),
            dma((1,)),
            dma((chunks,)),
            dma((1,)),
            dma((1,)),
            dma((chunks,)),
            dma((chunks, loops - 1)),
            dma((chunks,)),
            dma((1,)),
            dma((1,)),
        ],
        compiler_params=pltpu.CompilerParams(
            collective_id=0, has_side_effects=True, vmem_limit_bytes=60 * 2**20
        ),
    )(
        cand_owner.reshape(1, share),
        cand_row.reshape(1, share),
        coverage.reshape(n_docs // LANES, LANES),
        elem_weight.reshape(n_docs // LANES, LANES),
        doc_pool.reshape(pool_rows, width),
        elements.reshape(n_docs, width),
    )
    return out.reshape(1, 1, share)


def solution(mesh):
    slabs, loops = mesh.shape["slab"], mesh.shape["loop"]

    def whole(doc_pool, cand_owner, cand_row, elements, coverage, elem_weight):
        share = cand_row.shape[2]
        width = doc_pool.shape[3]
        n_docs = elements.shape[2]
        cap = max(2, 2 * share // slabs)
        dims = (
            slabs, loops, share, cap, CHUNKS, width // CHUNKS, min(512, n_docs),
            float(n_docs * slabs * loops), float(width) ** (-0.5),
        )
        placed = (
            P("slab", "loop", None, None),
            P("slab", "loop", None, None),
            P("slab", "loop", None),
            P("slab", "loop", None, None),
            P("slab", "loop", None),
            P("slab", "loop", None),
        )
        return jax.shard_map(
            functools.partial(body, dims), mesh=mesh, in_specs=placed,
            out_specs=P("slab", "loop", None), check_vma=False,
        )(doc_pool, cand_owner, cand_row, elements, coverage, elem_weight)

    return whole
```

```python
import functools

import jax
import jax.numpy as jnp
from jax import lax
from jax.experimental import pallas as pl
from jax.experimental.pallas import tpu as pltpu
from jax.sharding import PartitionSpec as P

MESH = pl.DeviceIdType.MESH
LANES = 128
SUB = 8
CHUNKS = 8
OWN_LEAD = 4
RING_LAG = 3
HOP_LAG = 2
LAST_LAG = 1


def kernel(
    dims,
    owner_ref, row_ref, cover_ref, weight_ref, pool_hbm, docs_hbm,
    out_ref,
    pool, docs, req_out, req_in, picked, fetched, cand, acc, part, terms,
    pool_sem, docs_sem, req_send, req_recv, pick_send, pick_recv,
    cand_send, relay_send, line_recv, ring_recv, pair_recv, term_send, term_recv,
):
    slabs, loops, share, cap, chunks, chunk, tile, total_docs, scale = dims
    lines = slabs // 2
    units = slabs * loops
    rows_pool = pool.shape[0]
    n_docs = docs.shape[0]
    slab = lax.axis_index("slab")
    loop = lax.axis_index("loop")
    line = slab // 2
    core = lax.rem(slab, 2)
    me = slab * loops + loop
    half = loops // 2
    reach_even, reach_odd = half, loops - 1 - half
    relayed = lines == 4

    def loop_of(pos):
        return jnp.where(pos < half, 2 * pos, 2 * (loops - 1 - pos) + 1)

    def pos_of(at):
        return jnp.where(lax.rem(at, 2) == 0, at // 2, loops - 1 - at // 2)

    here = pos_of(loop)
    ahead = loop_of(lax.rem(here + 1, loops))
    behind = loop_of(lax.rem(here + loops - 1, loops))

    pool_copy = pltpu.make_async_copy(pool_hbm, pool, pool_sem.at[0])
    docs_copy = pltpu.make_async_copy(docs_hbm, docs, docs_sem.at[0])

    barrier = pltpu.get_barrier_semaphore()

    def greet(device):
        pl.semaphore_signal(barrier, inc=1, device_id=device, device_id_type=MESH)

    for d in range(1, slabs):
        greet((lax.rem(slab + d, slabs), loop))
    for d in range(1, loops):
        greet((slab, lax.rem(loop + d, loops)))
    pool_copy.start()
    docs_copy.start()

    owner_row = owner_ref[...]
    row_row = row_ref[...]
    down = lax.broadcasted_iota(jnp.int32, (share, share), 0)
    across = lax.broadcasted_iota(jnp.int32, (share, share), 1)
    wide = jnp.broadcast_to(owner_row, (share, share)).astype(jnp.float32)
    owner_col = jnp.sum(jnp.where(down == across, wide, 0.0), axis=1, keepdims=True)
    rank_row = jnp.sum(
        jnp.where((owner_col == wide) & (down < across), 1.0, 0.0), axis=0, keepdims=True
    )
    owner_f = owner_row.astype(jnp.float32)
    asked_row = owner_f * SUB + rank_row
    slot_row = owner_f * cap + rank_row
    slot_col = jnp.sum(
        jnp.where(down == across, jnp.broadcast_to(slot_row, (share, share)), 0.0),
        axis=1, keepdims=True,
    )
    place = lax.broadcasted_iota(jnp.int32, (slabs * SUB, share), 0).astype(jnp.float32)
    asked = jnp.sum(
        jnp.where(place == asked_row, row_row.astype(jnp.float32), 0.0), axis=1, keepdims=True
    )
    req_out[...] = jnp.broadcast_to(asked, (slabs * SUB, LANES)).astype(jnp.int32).reshape(
        slabs, SUB, LANES
    )
    choose = jnp.where(
        slot_col == lax.broadcasted_iota(jnp.int32, (share, slabs * cap), 1).astype(jnp.float32),
        1.0, 0.0,
    ).astype(jnp.bfloat16)

    pl.semaphore_wait(barrier, slabs + loops - 2)

    def remote(src, dst, send, recv, device):
        return pltpu.make_async_remote_copy(
            src_ref=src, dst_ref=dst, send_sem=send, recv_sem=recv,
            device_id=device, device_id_type=MESH,
        )

    def settle(ref, sem):
        pltpu.make_async_copy(ref, ref, sem).wait()

    for d in range(1, slabs):
        other = lax.rem(slab + d, slabs)
        remote(
            req_out.at[other], req_in.at[slab], req_send.at[0], req_recv.at[0], (other, loop)
        ).start()
    req_in[slab] = req_out[slab]
    pool_copy.wait()
    settle(req_in.at[pl.ds(0, slabs - 1)], req_recv.at[0])

    wanted = req_in[...].reshape(slabs * SUB, LANES)
    lane = lax.broadcasted_iota(jnp.int32, (slabs * SUB, LANES), 1)
    pick = jnp.concatenate(
        [
            jnp.where(wanted == lane + b * LANES, 1.0, 0.0).astype(jnp.bfloat16)
            for b in range(rows_pool // LANES)
        ],
        axis=1,
    )

    def gather(k):
        rows = jnp.dot(
            pick, pool[:, k * chunk:(k + 1) * chunk], preferred_element_type=jnp.float32
        )
        for r in range(slabs):
            picked[k, r] = rows[r * SUB:r * SUB + cap].astype(jnp.bfloat16)
        for d in range(1, slabs):
            other = lax.rem(slab + d, slabs)
            remote(
                picked.at[k, other], fetched.at[k, slab], pick_send.at[0], pick_recv.at[k],
                (other, loop),
            ).start()
        fetched[k, slab] = picked[k, slab]

    def to_ring(k, block, e, way):
        slot = e - 1 if way == 0 else jnp.where(core == 0, reach_even, reach_odd) + e - 1
        remote(
            block, block, cand_send.at[0], ring_recv.at[k, slot],
            (slab, ahead if way == 0 else behind),
        ).start()

    def to_pair(k, pos):
        block = cand.at[k, core, pos]
        remote(
            block, block, cand_send.at[0], pair_recv.at[k], (2 * line + 1 - core, loop)
        ).start()

    edge = (line == 0) | (line == lines - 1)

    def own(k):
        settle(fetched.at[k, pl.ds(0, slabs - 1)], pick_recv.at[k])
        rows = jnp.concatenate(
            [fetched[k, o].astype(jnp.float32) for o in range(slabs)], axis=0
        ).astype(jnp.bfloat16)
        mine = jnp.dot(choose, rows, preferred_element_type=jnp.float32)
        cand[k, core, here, line] = mine.astype(jnp.bfloat16)
        block = cand.at[k, core, here, line]
        if relayed:
            targets = [
                jnp.where(edge, jnp.where(line == 0, 2, 1), lines - 1 - line),
                jnp.where(edge, jnp.where(line == 0, 1, 2), jnp.where(line == 1, 0, 3)),
            ]
        else:
            targets = [lax.rem(line + d, lines) for d in range(1, lines)]
        for to in targets:
            remote(
                block, block, cand_send.at[0], line_recv.at[k], (2 * to + core, loop)
            ).start()
        to_ring(k, block, 1, 0)
        to_ring(k, block, 1, 1)

    def column(k):
        settle(cand.at[k, 0, 0, pl.ds(0, lines - 1)], line_recv.at[k])
        if relayed:
            @pl.when(jnp.logical_not(edge))
            def _():
                block = cand.at[k, core, here, pl.ds(jnp.where(line == 1, 2, 0), 2)]
                remote(
                    block, block, relay_send.at[0], line_recv.at[k],
                    (2 * jnp.where(line == 1, 0, 3) + core, loop),
                ).start()
        for d in range(1, lines):
            block = cand.at[k, core, here, lax.rem(line + d, lines)]
            to_ring(k, block, 1, 0)
            to_ring(k, block, 1, 1)
        to_pair(k, here)

    def ring(k, e):
        for way in (0, 1):
            reach = (reach_even, reach_odd) if way == 0 else (reach_odd, reach_even)
            limit = jnp.where(core == 0, reach[0], reach[1])
            pos = lax.rem(here - e + loops if way == 0 else here + e, loops)
            block = cand.at[k, core, pos]

            def arrive(way=way, reach=reach, limit=limit, pos=pos, block=block):
                slot = e - 1 if way == 0 else jnp.where(core == 0, reach_even, reach_odd) + e - 1
                settle(block, ring_recv.at[k, slot])
                if e < min(reach):
                    to_ring(k, block, e + 1, way)
                elif e < max(reach):
                    @pl.when(e < limit)
                    def _():
                        to_ring(k, block, e + 1, way)
                to_pair(k, pos)

            if e <= min(reach):
                arrive()
            elif e <= max(reach):
                pl.when(e <= limit)(arrive)

    cover_cols = jnp.transpose(cover_ref[...])
    weight_cols = jnp.transpose(weight_ref[...])
    tiles = n_docs // tile

    def multiply(k, i):
        if k == 0 and i == 0:
            docs_copy.wait()
        share_all = cand[k].reshape(units * share, chunk)
        at = slice(i * tile, (i + 1) * tile)
        product = lax.dot_general(
            docs[at, k * chunk:(k + 1) * chunk], share_all, (((1,), (1,)), ((), ())),
            preferred_element_type=jnp.float32,
        )
        if k == 0:
            acc[at, :] = product
        elif k < chunks - 1:
            acc[at, :] += product
        else:
            scores = (acc[at, :] + product) * scale
            total = jnp.zeros((1, units * share), jnp.float32)
            for j in range(tile // LANES):
                col = i * (tile // LANES) + j
                s = scores[j * LANES:(j + 1) * LANES, :]
                gain = weight_cols[:, col:col + 1] * jnp.maximum(
                    s - cover_cols[:, col:col + 1], 0.0
                )
                total = total + jnp.sum(gain, axis=0, keepdims=True)
            return total

    for k in range(chunks):
        gather(k)
    for k in range(min(OWN_LEAD, chunks)):
        own(k)
    lags = [RING_LAG + HOP_LAG * (e - 1) for e in range(1, half + 1)]
    final = lags[-1] + LAST_LAG
    total = jnp.zeros((1, units * share), jnp.float32)
    for t in range(chunks + final):
        stages = []
        if t + OWN_LEAD < chunks:
            stages.append(functools.partial(own, t + OWN_LEAD))
        for e in range(1, half + 1):
            if 0 <= t - lags[e - 1] < chunks:
                stages.append(functools.partial(ring, t - lags[e - 1], e))
        if t < chunks:
            stages.append(functools.partial(column, t))
        done = t - final
        if done >= 0:
            settle(cand.at[done, 0], pair_recv.at[done])
        for n in range(max(tiles, len(stages))):
            if n < len(stages):
                stages[n]()
            if done >= 0 and n < tiles:
                gains = multiply(done, n)
                if gains is not None:
                    total = total + gains
    total = total / total_docs
    for r in range(units * share // LANES):
        part[r] = total[:, r * LANES:(r + 1) * LANES]

    def first_of(s, p):
        return ((lax.rem(s, 2) * loops + pos_of(p)) * lines + s // 2) * share

    for d in range(slabs):
        for e in range(loops):
            if d + e > 0:
                s, p = lax.rem(slab + d, slabs), lax.rem(loop + e, loops)
                remote(
                    part.at[first_of(s, p) // LANES], terms.at[me], term_send.at[0],
                    term_recv.at[0], (s, p),
                ).start()
    first = first_of(slab, loop)
    terms[me] = part[first // LANES]
    sent = 2 + (2 if relayed else lines - 1) + 2 * (lines - 1) + (loops - 3) * lines + loops * lines
    settle(docs.at[pl.ds(0, sent * share)], cand_send.at[0])
    if relayed:
        @pl.when(jnp.logical_not(edge))
        def _():
            settle(docs.at[pl.ds(0, 2 * share)], relay_send.at[0])
    settle(req_in.at[pl.ds(0, slabs - 1)], req_send.at[0])
    settle(picked.at[:, pl.ds(0, slabs - 1)], pick_send.at[0])
    settle(terms.at[pl.ds(0, units - 1)], term_recv.at[0])
    settle(terms.at[pl.ds(0, units - 1)], term_send.at[0])
    row = jnp.sum(terms[...], axis=0)
    mine = lax.broadcasted_iota(jnp.int32, (LANES, LANES), 0)
    to = lax.broadcasted_iota(jnp.int32, (LANES, LANES), 1)
    column_of = jnp.sum(
        jnp.where(mine == to, jnp.broadcast_to(row, (LANES, LANES)), 0.0), axis=1, keepdims=True
    )
    moved = jnp.sum(
        jnp.where(mine == to + lax.rem(first, LANES), column_of, 0.0), axis=0, keepdims=True
    )
    out_ref[...] = moved[:, :share]


def body(dims, doc_pool, cand_owner, cand_row, elements, coverage, elem_weight):
    slabs, loops, share, cap, chunks, chunk, tile, _, _ = dims
    pool_rows, width = doc_pool.shape[2:]
    n_docs = elements.shape[2]
    units = slabs * loops
    vmem = pl.BlockSpec(memory_space=pltpu.VMEM)
    hbm = pl.BlockSpec(memory_space=pl.ANY)
    dma = pltpu.SemaphoreType.DMA
    out = pl.pallas_call(
        functools.partial(kernel, dims),
        out_shape=jax.ShapeDtypeStruct((1, share), jnp.float32),
        in_specs=[vmem, vmem, vmem, vmem, hbm, hbm],
        out_specs=vmem,
        scratch_shapes=[
            pltpu.VMEM((pool_rows, width), jnp.bfloat16),
            pltpu.VMEM((n_docs, width), jnp.bfloat16),
            pltpu.VMEM((slabs, SUB, LANES), jnp.int32),
            pltpu.VMEM((slabs, SUB, LANES), jnp.int32),
            pltpu.VMEM((chunks, slabs, cap, chunk), jnp.bfloat16),
            pltpu.VMEM((chunks, slabs, cap, chunk), jnp.bfloat16),
            pltpu.VMEM((chunks, 2, loops, slabs // 2, share, chunk), jnp.bfloat16),
            pltpu.VMEM((n_docs, units * share), jnp.float32),
            pltpu.VMEM((units * share // LANES, 1, LANES), jnp.float32),
            pltpu.VMEM((units, 1, LANES), jnp.float32),
            dma((1,)),
            dma((1,)),
            dma((1,)),
            dma((1,)),
            dma((1,)),
            dma((chunks,)),
            dma((1,)),
            dma((1,)),
            dma((chunks,)),
            dma((chunks, loops - 1)),
            dma((chunks,)),
            dma((1,)),
            dma((1,)),
        ],
        compiler_params=pltpu.CompilerParams(
            collective_id=0, has_side_effects=True, vmem_limit_bytes=60 * 2**20
        ),
    )(
        cand_owner.reshape(1, share),
        cand_row.reshape(1, share),
        coverage.reshape(n_docs // LANES, LANES),
        elem_weight.reshape(n_docs // LANES, LANES),
        doc_pool.reshape(pool_rows, width),
        elements.reshape(n_docs, width),
    )
    return out.reshape(1, 1, share)


def solution(mesh):
    slabs, loops = mesh.shape["slab"], mesh.shape["loop"]

    def whole(doc_pool, cand_owner, cand_row, elements, coverage, elem_weight):
        share = cand_row.shape[2]
        width = doc_pool.shape[3]
        n_docs = elements.shape[2]
        cap = max(2, 2 * share // slabs)
        dims = (
            slabs, loops, share, cap, CHUNKS, width // CHUNKS, min(512, n_docs),
            float(n_docs * slabs * loops), float(width) ** (-0.5),
        )
        placed = (
            P("slab", "loop", None, None),
            P("slab", "loop", None, None),
            P("slab", "loop", None),
            P("slab", "loop", None, None),
            P("slab", "loop", None),
            P("slab", "loop", None),
        )
        return jax.shard_map(
            functools.partial(body, dims), mesh=mesh, in_specs=placed,
            out_specs=P("slab", "loop", None), check_vma=False,
        )(doc_pool, cand_owner, cand_row, elements, coverage, elem_weight)

    return whole
```
